32 devices in a mesh: dp: 8 (over y, x, core), tensor: 4 (over z).
Axes of the slice: x: 2, y: 2, z: 4, core: 2. Of those that a mesh axis runs over, the one named last changes fastest.
Arguments:
- tokens: bfloat16 [16, 1024, 768], P('dp', 'tensor'), may hold values from -6 to 6
- segments: int32 [16, 1024], P('dp', 'tensor'), may hold values from 0 to 15, as said below
- cotangent: bfloat16 [16, 1024, 768], P('dp', 'tensor'), may hold values from -6 to 6
- w_qkv: bfloat16 [768, 3, 768], P('dp', None, 'tensor'), may hold values from -0.21875 to 0.21875
- w_out: bfloat16 [768, 768], P('tensor', 'dp'), may hold values from -3.5 to 3.5
- w_gate_up: bfloat16 [768, 2, 3072], P('dp', None, 'tensor'), may hold values from -0.21875 to 0.21875
- w_down: bfloat16 [3072, 768], P('tensor', 'dp'), may hold values from -0.109375 to 0.109375
- norm_gain: bfloat16 [2, 768], P(None, 'dp'), may hold values from 0.099609375 to 1.8984375
- norm_bias: bfloat16 [2, 768], P(None, 'dp'), may hold values from -3 to 3
Outputs:
- layer_out: bfloat16 [16, 1024, 768], P('dp', 'tensor')
- input_grad: bfloat16 [16, 1024, 768], P('dp', 'tensor')
- grad_qkv: float32 [768, 3, 768], P('dp', None, 'tensor')
- grad_out: float32 [768, 768], P('tensor', 'dp')
- grad_gate_up: float32 [768, 2, 3072], P('dp', None, 'tensor')
- grad_down: float32 [3072, 768], P('tensor', 'dp')
- grad_gain: float32 [2, 768], P(None, ('dp', 'tensor'))
- grad_bias: float32 [2, 768], P(None, ('dp', 'tensor'))
The draws below stay inside these ranges and needn't reach their ends.
Inputs may be any that keep to these rules, and one draw needn't show every extreme that they name: `segments`: in each sequence the segment numbers start at 0 and never fall; every segment but a sequence's last holds 64 to 800 tokens; some sequence holds 16 documents.
All inputs are finite; a program needn't handle non-finite values.
Results may differ from the reference program's by a relative error of at most 0.025.
Values may be sent and summed in bfloat16 or wider, within the bound.
No kernel may reach another device: no remote copies, remote signals or barrier semaphores. Data moves between devices by JAX's collectives and lax.ppermute only.
A program may use at most 128 MiB of HBM per device.

```python
import math
import jax
import jax.numpy as jnp
from jax import lax

D = 768
H = 12
HD = 64
FF = 3072
SEQ_LEN = 1024
SEQS = 16


def draw_segments(key, part):
    shortest = SEQ_LEN // 16
    longest = SEQ_LEN * 25 // 32
    slot_count = SEQ_LEN // shortest + 2
    random_lengths = jax.random.randint(key, (SEQS, slot_count), shortest, longest + 1, dtype=jnp.int32)
    first_row = (jnp.arange(SEQS, dtype=jnp.int32) == 0)[:, None]
    doc_lengths = jnp.where(first_row, jnp.int32(shortest), random_lengths).astype(jnp.int32)
    doc_ends = jnp.cumsum(doc_lengths, axis=1)
    places = jnp.arange(SEQ_LEN, dtype=jnp.int32)
    passed = (doc_ends[:, None, :] <= places[None, :, None]).astype(jnp.int32)
    return jnp.sum(passed, axis=2).astype(jnp.int32)


def with_spikes(values, key, source, target, shards_of, factor):
    owner, partner = [(jnp.arange(values.shape[dim]) // (values.shape[dim] // shards_of)).reshape([-1 if axis == dim else 1 for axis in range(values.ndim)]) for dim in (source, target)]
    chosen = jax.random.permutation(key, shards_of)[partner]
    strong = (owner == chosen) | (owner == (partner + shards_of // 2) % shards_of)
    return jnp.where(strong, factor * values, values)


def block_levels(stream_key, dims, shards, smallest, high):
    gain, own = 1.0, jax.random.fold_in(stream_key, 6)
    for axis_at, parts in shards:
        draws = jnp.exp(jax.random.uniform(jax.random.fold_in(own, axis_at), (parts,), jnp.float32, smallest / len(shards), high / len(shards)))
        gain = gain * jnp.repeat(draws, dims[axis_at] // parts).reshape([-1 if axis == axis_at else 1 for axis in range(len(dims))])
    return gain


def scatter_about(stream_key, extent, scale, reach, pieces=(), kind=jnp.bfloat16):
    drawn = scale * jax.random.normal(stream_key, extent, jnp.float32)
    if pieces:
        drawn = drawn * block_levels(stream_key, extent, pieces, -0.22, 0.18)
    return jnp.clip(drawn, -reach, reach).astype(kind)


def gaussian_with(key, extent, width, limit, cuts, heavy, held_as=jnp.bfloat16):
    entries = width * jax.random.normal(key, extent, jnp.float32)
    if cuts:
        entries = entries * block_levels(key, extent, cuts, -0.22, 0.18)
    return jnp.clip(with_spikes(entries, jax.random.fold_in(key, 3), *heavy), -limit, limit).astype(held_as)


def setup_inputs(seed: int = 0) -> dict:
    key_list = jax.random.split(jax.random.key(seed), 10)
    tokens = gaussian_with(key_list[0], (SEQS, SEQ_LEN, D), 1.0, 6.0, ((0, 8), (1, 4)), (0, 2, 8, 2.0))
    segments = draw_segments(jax.random.fold_in(key_list[9], 71), 0)
    cotangent = gaussian_with(key_list[2], (SEQS, SEQ_LEN, D), 1.0, 6.0, ((0, 8), (1, 4)), (0, 2, 8, 2.0))
    w_qkv = scatter_about(key_list[3], (D, 3, D), D ** -0.5, 0.21875, ((0, 8), (2, 4)))
    w_out = scatter_about(key_list[4], (D, D), (D // 256) ** -0.5, 3.5, ((0, 4), (1, 8)))
    w_gate_up = scatter_about(key_list[5], (D, 2, FF), D ** -0.5, 0.21875, ((0, 8), (2, 4)))
    w_down = scatter_about(key_list[6], (FF, D), FF ** -0.5, 0.109375, ((0, 4), (1, 8)))
    norm_gain = jnp.clip(1.0 + 0.18 * jax.random.normal(key_list[7], (2, D), jnp.float32), 0.099609375, 1.8984375).astype(jnp.bfloat16)
    norm_bias = scatter_about(key_list[8], (2, D), 0.5, 3.0, ((1, 8),))
    return {"tokens": tokens, "segments": segments, "cotangent": cotangent, "w_qkv": w_qkv, "w_out": w_out, "w_gate_up": w_gate_up, "w_down": w_down, "norm_gain": norm_gain, "norm_bias": norm_bias}


@jax.custom_vjp
def low(v):
    return lax.optimization_barrier(v.astype(jnp.bfloat16)).astype(jnp.float32)

@jax.custom_vjp
def low_back(v):
    return v

def low_keep(v):
    return (low(v), None)

def low_pass(kept, grad):
    return (grad,)

def back_keep(v):
    return (v, None)

def back_low(kept, grad):
    return (low(grad),)
low.defvjp(low_keep, low_pass)
low_back.defvjp(back_keep, back_low)
highest = lax.Precision.HIGHEST
rotary_base = 1000.0
norm_eps = 1e-06

def matmul(left_side, right_side):
    return jnp.dot(left_side, right_side, precision=highest)

def rotary_tables(segment_ids, head_size):
    length = segment_ids.shape[0]
    places = jnp.arange(length, dtype=jnp.int32)
    change = jnp.concatenate([jnp.ones((1,), dtype=jnp.bool_), segment_ids[1:] != segment_ids[:-1]])
    starts = lax.cummax(jnp.where(change, places, 0), axis=0)
    offsets = (places - starts).astype(jnp.float32)
    inverse_freq = rotary_base ** (-jnp.arange(0, head_size, 2, dtype=jnp.float32) / head_size)
    angles = offsets[:, None] * inverse_freq[None, :]
    return (jnp.cos(angles), jnp.sin(angles))

def rotate(values, cosine, sines):
    half_size = values.shape[-1] // 2
    front_half = values[..., :half_size]
    back_half = values[..., half_size:]
    cos_rows = cosine[:, None, :]
    sin_rows = sines[:, None, :]
    return jnp.concatenate([front_half * cos_rows - back_half * sin_rows, back_half * cos_rows + front_half * sin_rows], axis=-1)

def layer_norm(inputs, gain_row, bias_row):
    center = inputs - lax.optimization_barrier(jnp.mean(inputs, axis=-1, keepdims=True))
    spread = lax.optimization_barrier(jnp.mean(center * center, axis=-1, keepdims=True))
    return center * lax.rsqrt(spread + norm_eps) * gain_row + bias_row

def attend_block(query_block, segment_block, key_all, value_all, segment_all):
    raw_scores = jnp.einsum('qhd,khd->hqk', query_block, key_all, precision=highest)
    scores = low_back(raw_scores * HD ** (-0.5))
    same_doc = segment_block[:, None] == segment_all[None, :]
    masked = jnp.where(same_doc[None], scores, -1e+30)
    top_score = lax.optimization_barrier(jnp.max(masked, axis=-1, keepdims=True))
    log_total = top_score + jnp.log(lax.optimization_barrier(jnp.sum(jnp.exp(masked - top_score), axis=-1, keepdims=True)))
    attn_probs = low(jnp.exp(masked - log_total))
    return jnp.einsum('hqk,khd->qhd', attn_probs, value_all, precision=highest)

def forward_one(tokens_row, segment_row, w_qkv, w_out, w_gate_up, w_down, norm_gain, norm_bias):
    length = tokens_row.shape[0]
    cosine, sines = rotary_tables(segment_row, HD)
    mixed = low_back(matmul(tokens_row, w_qkv.reshape(D, 3 * D))).reshape(length, 3, H, HD)
    query_all = low(rotate(mixed[:, 0], cosine, sines))
    key_all = low(rotate(mixed[:, 1], cosine, sines))
    value_all = low(mixed[:, 2])
    block_rows = min(512, length)
    block_count = length // block_rows
    query_blocks = query_all.reshape(block_count, block_rows, H, HD)
    segment_blocks = segment_row.reshape(block_count, block_rows)

    def one_block(block_pair):
        return attend_block(block_pair[0], block_pair[1], key_all, value_all, segment_row)
    heads_out = lax.map(jax.checkpoint(one_block), (query_blocks, segment_blocks)).reshape(length, D)
    joined = low(low_back(heads_out))
    attn_branch = low_back(matmul(joined, w_out))
    first = layer_norm(tokens_row + attn_branch, norm_gain[0], norm_bias[0])
    gate_up = low_back(matmul(low(first), w_gate_up.reshape(D, 2 * FF))).reshape(length, 2, FF)
    hidden = low(jax.nn.silu(gate_up[:, 0]) * gate_up[:, 1])
    mlp_branch = low_back(matmul(hidden, w_down))
    return layer_norm(first + mlp_branch, norm_gain[1], norm_bias[1])

def reference(tokens, segments, cotangent, w_qkv, w_out, w_gate_up, w_down, norm_gain, norm_bias):
    group_size = math.gcd(SEQS, max(1, 4096 // SEQ_LEN))
    group_count = SEQS // group_size
    weights = tuple((matrix.astype(jnp.float32) for matrix in (w_qkv, w_out, w_gate_up, w_down, norm_gain, norm_bias)))

    def one_group(running, batch_in):
        group_tokens, group_segments, group_cot = batch_in

        def forward_group(inputs, *params):
            return jax.vmap(forward_one, in_axes=(0, 0, None, None, None, None, None, None))(inputs, group_segments, *params)
        outputs, pullback = jax.vjp(forward_group, group_tokens.astype(jnp.float32), *weights)
        grads_all = pullback(group_cot.astype(jnp.float32))
        running = tuple((before + added for before, added in zip(running, grads_all[1:])))
        return (running, (outputs.astype(jnp.bfloat16), grads_all[0].astype(jnp.bfloat16)))
    start_sums = tuple((jnp.zeros(matrix.shape, jnp.float32) for matrix in weights))
    batches = (tokens.reshape(group_count, group_size, SEQ_LEN, D), segments.reshape(group_count, group_size, SEQ_LEN), cotangent.reshape(group_count, group_size, SEQ_LEN, D))
    sums_out, stacked = lax.scan(one_group, start_sums, batches)
    layer_out = stacked[0].reshape(SEQS, SEQ_LEN, D)
    input_grad = stacked[1].reshape(SEQS, SEQ_LEN, D)
    return (layer_out, input_grad, sums_out[0], sums_out[1], sums_out[2], sums_out[3], sums_out[4], sums_out[5])
```

```python
import functools

import jax
import jax.numpy as jnp
from jax import lax
from jax.experimental import pallas as pl
from jax.experimental.pallas import tpu as pltpu
from jax.sharding import Mesh, PartitionSpec as P

HD = 64
BF = jnp.bfloat16
F32 = jnp.float32

rotary_base = 1000.0
norm_eps = 1e-06


CHIP = ("hi", "y", "x", "z")


def dot(a, b, ca, cb):
    return lax.dot_general(a, b, (((ca,), (cb,)), ((), ())), preferred_element_type=F32)


def swap_core(v):
    return lax.ppermute(v, "c", [(0, 1), (1, 0)])


def flip(v, name):
    if name == "b":
        return lax.ppermute(v, "z", [(i, i ^ 1) for i in range(4)])
    if name == "k":
        return lax.ppermute(v, "z", [(i, i ^ 2) for i in range(4)])
    return lax.ppermute(v, name, [(0, 1), (1, 0)])


def cross(v):
    perm = [(c * 4 + 2 * k + b, b * 4 + 2 * k + c) for c in range(2) for k in range(2) for b in range(2)]
    return lax.ppermute(v, ("c", "z"), perm)


def spread_perm(r):
    pairs = []
    for c in range(2):
        for z in range(4):
            pairs.append((c * 4 + z, (z & 1) * 4 + 2 * c + (r ^ (z >> 1))))
    return pairs


def to_chip(parts, z, c):
    high = z >> 1
    got = [
        lax.ppermute(lax.dynamic_index_in_dim(parts, high ^ r, 0, False), ("c", "z"), spread_perm(r))
        for r in range(2)
    ]
    odd = (z & 1) == 1
    mine = jnp.stack([jnp.where(odd, got[1], got[0]), jnp.where(odd, got[0], got[1])])
    other = swap_core(mine)
    first = c == 0
    both = jnp.stack([jnp.where(first, mine, other), jnp.where(first, other, mine)], axis=1)
    return both.reshape((4,) + both.shape[2:])


def from_chip(mine, z):
    sent = []
    for r in range(2):
        back = [(d, s) for s, d in spread_perm(r)]
        sent.append(lax.ppermute(lax.dynamic_index_in_dim(mine, (z & 1) ^ r, 0, False), ("c", "z"), back))
    high = (z >> 1) == 1
    return jnp.stack([jnp.where(high, sent[1], sent[0]), jnp.where(high, sent[0], sent[1])])


def attend_kernel(x_ref, w_ref, cos_ref, sin_ref, segc_ref, segr_ref,
                  q_ref, qt_ref, k_ref, kt_ref, v_ref, lse_ref, jn_ref, out_ref,
                  vt_ref, jt_ref, bias_ref, acc_ref, *, heads, tile):
    step = pl.program_id(0)
    rows, width = x_ref.shape
    part = heads * HD
    w = w_ref[...].reshape(width, 4 * part)
    mixed = dot(w[:, : 3 * part], x_ref[...], 0, 1)
    cosine, sines = cos_ref[...], sin_ref[...]

    def turn(m):
        out = []
        for h in range(heads):
            u1 = m[h * HD : h * HD + HD // 2]
            u2 = m[h * HD + HD // 2 : (h + 1) * HD]
            out += [u1 * cosine - u2 * sines, u2 * cosine + u1 * sines]
        return jnp.concatenate(out, axis=0)

    qt = (turn(mixed[:part]) * (HD ** -0.5)).astype(BF)
    kt = turn(mixed[part : 2 * part]).astype(BF)
    vt = mixed[2 * part :].astype(BF)
    qt_ref[...] = qt[None]
    kt_ref[...] = kt[None]
    vt_ref[...] = vt
    q_ref[...] = qt.T[None]
    k_ref[...] = kt.T[None]
    v_ref[...] = vt.T[None]
    row_head = lax.broadcasted_iota(jnp.int32, (part, tile), 0) // HD

    def one_tile(t, carry):
        at = t * tile
        bias_ref[...] = jnp.where(segc_ref[...] == segr_ref[:, pl.ds(at, tile)], 0.0, -1e30)
        qtile = qt_ref[0, :, pl.ds(at, tile)]
        for h in range(heads):
            s = dot(k_ref[0], jnp.where(row_head == h, qtile, jnp.zeros_like(qtile)), 1, 0) + bias_ref[...]
            top = jnp.max(s, axis=0, keepdims=True)
            e = jnp.exp(s - top)
            total = jnp.sum(e, axis=0, keepdims=True)
            p = (e * (1.0 / total)).astype(BF)
            jt_ref[h * HD : (h + 1) * HD, pl.ds(at, tile)] = dot(vt_ref[h * HD : (h + 1) * HD, :], p, 1, 0).astype(BF)
            lse_ref[0, h : h + 1, pl.ds(at, tile)] = top + jnp.log(total)
        return carry

    for t in range(rows // tile):
        one_tile(t, 0)
    jn = jt_ref[...].T
    jn_ref[...] = jn[None]
    part_out = dot(jn, w[:, 3 * part :], 1, 1)

    @pl.when(step == 0)
    def _():
        acc_ref[...] = part_out

    @pl.when(step == pl.num_programs(0) - 1)
    def _():
        out_ref[...] = (acc_ref[...] + part_out).astype(BF)


def attend_back_kernel(ag_ref, x_ref, w_ref, cos_ref, sin_ref, segc_ref, segr_ref,
                       q_ref, qt_ref, k_ref, kt_ref, v_ref, lse_ref, jn_ref,
                       g_ref, out_ref,
                       jg_ref, jgt_ref, dqt_ref, dk_ref, dv_ref, bias_ref, acc_ref, *, heads, tile):
    step = pl.program_id(0)
    rows, width = x_ref.shape
    part = heads * HD
    w = w_ref[...].reshape(width, 4 * part)
    ag = ag_ref[...]
    jg = dot(ag, w[:, 3 * part :], 1, 0).astype(BF)
    jg_ref[...] = jg
    jgt_ref[...] = jg.T
    dk_ref[...] = jnp.zeros_like(dk_ref)
    dv_ref[...] = jnp.zeros_like(dv_ref)
    row_head = lax.broadcasted_iota(jnp.int32, (part, tile), 0) // HD
    col_head = lax.broadcasted_iota(jnp.int32, (tile, part), 1) // HD

    def one_tile(t, carry):
        at = t * tile
        bias_ref[...] = jnp.where(segc_ref[...] == segr_ref[:, pl.ds(at, tile)], 0.0, -1e30)
        qtt = qt_ref[0, :, pl.ds(at, tile)]
        jgt = jgt_ref[:, pl.ds(at, tile)]
        qtile = q_ref[0, pl.ds(at, tile), :]
        jgtile = jg_ref[pl.ds(at, tile), :]
        none_t, none = jnp.zeros_like(qtt), jnp.zeros_like(qtile)
        for h in range(heads):
            s = dot(k_ref[0], jnp.where(row_head == h, qtt, none_t), 1, 0) + bias_ref[...]
            p = jnp.exp(s - lse_ref[0, h : h + 1, pl.ds(at, tile)])
            dp = dot(v_ref[0], jnp.where(row_head == h, jgt, none_t), 1, 0)
            inner = jnp.sum(p * dp, axis=0, keepdims=True)
            ds = (p * (dp - inner)).astype(BF)
            dv_ref[...] += dot(p.astype(BF), jnp.where(col_head == h, jgtile, none), 1, 0)
            dk_ref[...] += dot(ds, jnp.where(col_head == h, qtile, none), 1, 0)
            dqt_ref[h * HD : (h + 1) * HD, pl.ds(at, tile)] = dot(kt_ref[0, h * HD : (h + 1) * HD, :], ds, 1, 0)
        return carry

    for t in range(rows // tile):
        one_tile(t, 0)
    cosine, sines = cos_ref[...], sin_ref[...]

    def turn_back(m):
        out = []
        for h in range(heads):
            g1 = m[h * HD : h * HD + HD // 2]
            g2 = m[h * HD + HD // 2 : (h + 1) * HD]
            out += [g1 * cosine + g2 * sines, g2 * cosine - g1 * sines]
        return jnp.concatenate(out, axis=0)

    dmt = jnp.concatenate(
        [turn_back(dqt_ref[...] * (HD ** -0.5)), turn_back(dk_ref[...].T), dv_ref[...].T], axis=0
    ).astype(BF)
    dm = dmt.T
    part_out = dot(dm, w[:, : 3 * part], 1, 1)
    g_qkv = dot(x_ref[...], dm, 0, 0)
    g_out = dot(ag, jn_ref[0], 0, 0)
    g_ref[...] = jnp.concatenate([g_qkv, g_out], axis=1).astype(BF)[None]

    @pl.when(step == 0)
    def _():
        acc_ref[...] = part_out

    @pl.when(step == pl.num_programs(0) - 1)
    def _():
        out_ref[...] = (acc_ref[...] + part_out).astype(BF)


def normed_rows(v):
    center = v - jnp.mean(v, axis=-1, keepdims=True)
    inv = lax.rsqrt(jnp.mean(center * center, axis=-1, keepdims=True) + norm_eps)
    return center * inv, inv


def norm_back(g, n, inv, gain):
    scaled = g * gain
    one = jnp.mean(scaled, axis=-1, keepdims=True)
    two = jnp.mean(scaled * n, axis=-1, keepdims=True)
    return inv * (scaled - one - n * two)


def mlp_kernel(x_ref, pa_ref, pb_ref, gain_ref, bias_ref, wg_ref, wu_ref, wd_ref,
               first_ref, low_ref, gate_ref, up_ref, hid_ref, out_ref, acc_ref, *, tile):
    step = pl.program_id(0)
    rows, width = x_ref.shape

    @pl.when(step == 0)
    def _():
        def one(t, carry):
            at = pl.ds(pl.multiple_of(t * tile, tile), tile)
            v = x_ref[at, :].astype(F32) + pa_ref[at, :].astype(F32) + pb_ref[at, :].astype(F32)
            n, _ = normed_rows(v)
            first = n * gain_ref[0:1, :] + bias_ref[0:1, :]
            first_ref[at, :] = first
            low_ref[at, :] = first.astype(BF)
            return carry

        lax.fori_loop(0, rows // tile, one, 0)

    def one_tile(t, carry):
        at = pl.ds(pl.multiple_of(t * tile, tile), tile)
        low = low_ref[at, :]
        gate = dot(low, wg_ref[...].reshape(width, -1), 1, 0)
        up = dot(low, wu_ref[...].reshape(width, -1), 1, 0)
        hid = (gate * (1.0 / (1.0 + jnp.exp(-gate))) * up).astype(BF)
        gate_ref[0, at, :] = gate.astype(BF)
        up_ref[0, at, :] = up.astype(BF)
        hid_ref[0, at, :] = hid
        got = dot(hid, wd_ref[...].reshape(width, -1), 1, 1)

        @pl.when(step == 0)
        def _():
            acc_ref[at, :] = got

        @pl.when(step == pl.num_programs(0) - 1)
        def _():
            out_ref[at, :] = (acc_ref[at, :] + got).astype(BF)

        return carry

    lax.fori_loop(0, rows // tile, one_tile, 0)


def mlp_back_kernel(first_ref, pa_ref, pb_ref, cot_ref, gain_ref, bias_ref, wg_ref, wu_ref, wd_ref,
                    gate_ref, up_ref, hid_ref,
                    lay_ref, gs_ref, gg_ref, ug_ref, gd_ref, sums_ref, out_ref, bg_ref, acc_ref, *, tile):
    step = pl.program_id(0)
    rows, width = first_ref.shape

    @pl.when(step == 0)
    def _():
        sums_ref[...] = jnp.zeros_like(sums_ref)

        def one(t, carry):
            at = pl.ds(pl.multiple_of(t * tile, tile), tile)
            v = first_ref[at, :] + pa_ref[at, :].astype(F32) + pb_ref[at, :].astype(F32)
            n, inv = normed_rows(v)
            lay_ref[at, :] = (n * gain_ref[1:2, :] + bias_ref[1:2, :]).astype(BF)
            cot = cot_ref[at, :].astype(F32)
            gs = norm_back(cot, n, inv, gain_ref[1:2, :])
            gs_ref[at, :] = gs
            bg_ref[at, :] = gs.astype(BF)
            sums_ref[0:1, :] += jnp.sum(cot * n, axis=0, keepdims=True)
            sums_ref[1:2, :] += jnp.sum(cot, axis=0, keepdims=True)
            return carry

        lax.fori_loop(0, rows // tile, one, 0)

    gd_ref[...] = dot(bg_ref[...], hid_ref[0], 0, 0).astype(BF)[None]

    def one_tile(t, carry):
        at = pl.ds(pl.multiple_of(t * tile, tile), tile)
        hg = dot(bg_ref[at, :], wd_ref[...].reshape(width, -1), 1, 0)
        gate = gate_ref[0, at, :].astype(F32)
        up = up_ref[0, at, :].astype(F32)
        s = 1.0 / (1.0 + jnp.exp(-gate))
        gg = (hg * up * s * (1.0 + gate * (1.0 - s))).astype(BF)
        ug = (hg * gate * s).astype(BF)
        gg_ref[0, at, :] = gg
        ug_ref[0, at, :] = ug
        got = dot(gg, wg_ref[...].reshape(width, -1), 1, 1) + dot(ug, wu_ref[...].reshape(width, -1), 1, 1)

        @pl.when(step == 0)
        def _():
            acc_ref[at, :] = got

        @pl.when(step == pl.num_programs(0) - 1)
        def _():
            out_ref[at, :] = (acc_ref[at, :] + got).astype(BF)

        return carry

    lax.fori_loop(0, rows // tile, one_tile, 0)


def wgrad_kernel(a_ref, b_ref, g_ref):
    g_ref[...] = dot(a_ref[...], b_ref[0], 0, 0).astype(BF)[None]


def first_back_kernel(x_ref, pa_ref, pb_ref, gs_ref, fa_ref, fb_ref, gain_ref, gf_ref, ag_ref, sums_ref, *, tile):
    rows, width = x_ref.shape
    sums_ref[...] = jnp.zeros_like(sums_ref)

    def one(t, carry):
        at = pl.ds(pl.multiple_of(t * tile, tile), tile)
        v = x_ref[at, :].astype(F32) + pa_ref[at, :].astype(F32) + pb_ref[at, :].astype(F32)
        n, inv = normed_rows(v)
        fg = gs_ref[at, :] + fa_ref[at, :].astype(F32) + fb_ref[at, :].astype(F32)
        gf = norm_back(fg, n, inv, gain_ref[0:1, :])
        gf_ref[at, :] = gf
        ag_ref[at, :] = gf.astype(BF)
        sums_ref[0:1, :] += jnp.sum(fg * n, axis=0, keepdims=True)
        sums_ref[1:2, :] += jnp.sum(fg, axis=0, keepdims=True)
        return carry

    lax.fori_loop(0, rows // tile, one, 0)


def whole(shape):
    return pl.BlockSpec(shape, lambda k: (0,) * len(shape), pipeline_mode=pl.Buffered(1))


def keep(shape):
    return pl.BlockSpec(shape, lambda k: (0,) * len(shape))


def per_k(shape):
    return pl.BlockSpec((1,) + shape, lambda k: (k,) + (0,) * len(shape))


PARAMS = pltpu.CompilerParams(vmem_limit_bytes=60 * 1024 * 1024)


def reduce_chips(grad, order, names):
    dims = ["k", "hi", "y", "x", "b"]
    for name in order:
        at = dims.index(name)
        i = names[name]
        mine = lax.dynamic_index_in_dim(grad, i, at, False)
        sent = lax.dynamic_index_in_dim(grad, 1 - i, at, False)
        grad = mine + flip(sent, name)
        dims.pop(at)
    if grad.shape[0] > 1:
        grad = lax.psum_scatter(grad, "hi", scatter_dimension=0, tiled=True)
    return cross(grad[0])


def per_device(tokens, segments, cotangent, w_qkv, w_out, w_gate_up, w_down, norm_gain, norm_bias):
    z = lax.axis_index("z")
    c = lax.axis_index("c")
    names = {"y": lax.axis_index("y"), "x": lax.axis_index("x"), "k": z >> 1, "b": z & 1}
    his = lax.axis_size("hi")
    quarter, width = tokens.shape[1], tokens.shape[2]
    rows = 4 * quarter
    share = w_qkv.shape[0]
    part = w_qkv.shape[2]
    heads = part // HD
    hidden = w_gate_up.shape[2]
    full = 4 * part
    assert full == width and hidden == width
    chips = his * 4

    packed = jnp.concatenate(
        [w_qkv.reshape(share, 3 * part), w_out.T, w_gate_up.reshape(share, 2 * hidden), w_down.T], axis=1
    )
    packed = cross(packed)
    norms = jnp.concatenate([norm_gain, norm_bias], axis=0)
    norm_all = lax.all_gather(norms, ("hi", "y", "x", "c"), axis=1, tiled=True).astype(F32)
    gain, bias = norm_all[:2], norm_all[2:]

    seg_rows = jnp.pad(segments.astype(BF)[:, None, :], ((0, 0), (0, 15), (0, width - quarter)))
    whole_in = to_chip(jnp.concatenate([tokens, seg_rows], axis=1), z, c)
    x = whole_in[:, :quarter].reshape(rows, width)
    seg = whole_in[:, quarter, :quarter].reshape(rows).astype(jnp.int32)
    cot = to_chip(cotangent, z, c).reshape(rows, width)

    gathered = lax.all_gather(packed, CHIP, axis=0, tiled=False)
    gathered = gathered.reshape(chips, 2, 2 * share, -1)
    if (2 * share) % 16:
        gathered = gathered.transpose(1, 0, 2, 3).reshape(1, 2, width, -1)
    blocks, inner = gathered.shape[0], gathered.shape[2]

    def weight(n):
        return pl.BlockSpec((blocks, 1, inner, width), lambda k: (0, k, 0, n))

    places = jnp.arange(rows, dtype=jnp.int32)
    change = jnp.concatenate([jnp.ones((1,), dtype=jnp.bool_), seg[1:] != seg[:-1]])
    starts = lax.cummax(jnp.where(change, places, 0), axis=0)
    offsets = (places - starts).astype(F32)
    inverse_freq = rotary_base ** (-jnp.arange(0, HD, 2, dtype=F32) / HD)
    angles = inverse_freq[:, None] * offsets[None, :]
    cosine, sines = jnp.cos(angles), jnp.sin(angles)
    seg_col, seg_row = seg[:, None], seg[None, :]

    act = jax.ShapeDtypeStruct((rows, width), BF)
    act32 = jax.ShapeDtypeStruct((rows, width), F32)
    head_rows = jax.ShapeDtypeStruct((2, rows, part), BF)
    head_cols = jax.ShapeDtypeStruct((2, part, rows), BF)
    tile = min(256, rows)
    tables = [keep((HD // 2, rows)), keep((HD // 2, rows)), keep((rows, 1)), keep((1, rows))]

    q, qt, k, kt, v, lse, joined, branch = pl.pallas_call(
        functools.partial(attend_kernel, heads=heads, tile=tile),
        grid=(2,),
        in_specs=[whole((rows, width)), weight(0)] + tables,
        out_specs=[per_k((rows, part)), per_k((part, rows)), per_k((rows, part)), per_k((part, rows)),
                   per_k((rows, part)), per_k((8, rows)), per_k((rows, part)), keep((rows, width))],
        out_shape=[head_rows, head_cols, head_rows, head_cols, head_rows,
                   jax.ShapeDtypeStruct((2, 8, rows), F32), head_rows, act],
        scratch_shapes=[pltpu.VMEM((part, rows), BF), pltpu.VMEM((part, rows), BF),
                        pltpu.VMEM((rows, tile), F32), pltpu.VMEM((rows, width), F32)],
        compiler_params=PARAMS,
        name="attend",
    )(x, gathered, cosine, sines, seg_col, seg_row)
    branch_other = swap_core(branch)

    hid_shape = jax.ShapeDtypeStruct((2, rows, hidden), BF)
    row_spec, two = whole((rows, width)), keep((2, width))
    first, first_low, gate, up, hid, mlp = pl.pallas_call(
        functools.partial(mlp_kernel, tile=tile),
        grid=(2,),
        in_specs=[row_spec, row_spec, row_spec, two, two, weight(1), weight(2), weight(3)],
        out_specs=[row_spec, row_spec, per_k((rows, hidden)), per_k((rows, hidden)), per_k((rows, hidden)), row_spec],
        out_shape=[act32, act, hid_shape, hid_shape, hid_shape, act],
        scratch_shapes=[pltpu.VMEM((rows, width), F32)],
        compiler_params=PARAMS,
        name="mlp",
    )(x, branch, branch_other, gain, bias, gathered, gathered, gathered)
    mlp_other = swap_core(mlp)

    grad_shape = jax.ShapeDtypeStruct((2, width, width), BF)
    sum_shape = jax.ShapeDtypeStruct((2, width), F32)
    layer, grad_second, gate_grad, up_grad, g_down, sums_two, first_part = pl.pallas_call(
        functools.partial(mlp_back_kernel, tile=tile),
        grid=(2,),
        in_specs=[row_spec, row_spec, row_spec, row_spec, two, two, weight(1), weight(2), weight(3)]
        + [per_k((rows, hidden))] * 3,
        out_specs=[row_spec, row_spec, per_k((rows, hidden)), per_k((rows, hidden)), per_k((width, hidden)), two, row_spec],
        out_shape=[act, act32, hid_shape, hid_shape, grad_shape, sum_shape, act],
        scratch_shapes=[pltpu.VMEM((rows, width), BF), pltpu.VMEM((rows, width), F32)],
        compiler_params=PARAMS,
        name="mlp_back",
    )(first, mlp, mlp_other, cot, gain, bias, gathered, gathered, gathered, gate, up, hid)
    first_other = swap_core(first_part)

    def wgrad(a, b):
        return pl.pallas_call(
            wgrad_kernel,
            grid=(2,),
            in_specs=[row_spec, per_k((rows, hidden))],
            out_specs=per_k((width, hidden)),
            out_shape=grad_shape,
            compiler_params=PARAMS,
            name="wgrad",
        )(a, b)

    def split(g):
        return g.reshape(2, his, 2, 2, 2, share, width)

    down_done = reduce_chips(split(g_down), "xybk", names)
    g_gate = wgrad(first_low, gate_grad)
    g_up = wgrad(first_low, up_grad)
    gate_done = reduce_chips(split(g_gate), "yxbk", names)
    up_done = reduce_chips(split(g_up), "xybk", names)

    row1 = pl.BlockSpec((rows, width), lambda: (0, 0))
    two1 = pl.BlockSpec((2, width), lambda: (0, 0))
    grad_first, attn_grad, sums_one = pl.pallas_call(
        functools.partial(first_back_kernel, tile=tile),
        in_specs=[row1] * 6 + [two1],
        out_specs=[row1, row1, two1],
        out_shape=[act32, act, sum_shape],
        compiler_params=PARAMS,
        name="first_back",
    )(x, branch, branch_other, grad_second, first_part, first_other, gain)

    g_qkvo, input_part = pl.pallas_call(
        functools.partial(attend_back_kernel, heads=heads, tile=tile),
        grid=(2,),
        in_specs=[row_spec, row_spec, weight(0)] + tables
        + [per_k((rows, part)), per_k((part, rows)), per_k((rows, part)), per_k((part, rows)),
           per_k((rows, part)), per_k((8, rows)), per_k((rows, part))],
        out_specs=[per_k((width, width)), keep((rows, width))],
        out_shape=[grad_shape, act],
        scratch_shapes=[pltpu.VMEM((rows, part), BF), pltpu.VMEM((part, rows), BF), pltpu.VMEM((part, rows), F32),
                        pltpu.VMEM((rows, part), F32), pltpu.VMEM((rows, part), F32),
                        pltpu.VMEM((rows, tile), F32), pltpu.VMEM((rows, width), F32)],
        compiler_params=PARAMS,
        name="attend_back",
    )(attn_grad, x, gathered, cosine, sines, seg_col, seg_row, q, qt, k, kt, v, lse, joined)
    qkvo_done = reduce_chips(split(g_qkvo), "yxbk", names)

    def pick(v, which):
        return lax.dynamic_index_in_dim(v.reshape(2, 2, quarter, width), which, 1, False)

    layer_out = from_chip(pick(layer, c), z)
    input_other = swap_core(pick(input_part, 1 - c))
    input_mine = (pick(grad_first, c) + pick(input_part, c).astype(F32) + input_other.astype(F32)).astype(BF)
    input_grad = from_chip(input_mine, z)

    sums = jnp.concatenate([sums_one, sums_two], axis=0)
    for name in ("x", "y", "b", "k"):
        sums = sums + flip(sums, name)
    if his > 1:
        sums = lax.psum(sums, "hi")
    own = width // (lax.axis_size("hi") * 32)
    device = ((lax.axis_index("hi") * 2 + names["y"]) * 2 + names["x"]) * 2 + c
    sums = lax.dynamic_slice_in_dim(sums, (device * 4 + z) * own, own, 1)
    gain_grad = jnp.stack([sums[0], sums[2]])
    bias_grad = jnp.stack([sums[1], sums[3]])

    qkvo = qkvo_done.astype(F32)
    return (
        layer_out,
        input_grad,
        qkvo[:, : 3 * part].reshape(share, 3, part),
        qkvo[:, 3 * part :].T,
        jnp.stack([gate_done, up_done], axis=1).astype(F32),
        down_done.astype(F32).T,
        gain_grad,
        bias_grad,
    )


def solution(mesh):
    dp, tensor = mesh.shape["dp"], mesh.shape["tensor"]
    assert dp % 8 == 0 and tensor == 4
    grid = Mesh(mesh.devices.reshape(dp // 8, 2, 2, 2, tensor), ("hi", "y", "x", "c", "z"))
    dps = ("hi", "y", "x", "c")
    return jax.shard_map(
        per_device,
        mesh=grid,
        in_specs=(
            P(dps, "z", None),
            P(dps, "z"),
            P(dps, "z", None),
            P(dps, None, "z"),
            P("z", dps),
            P(dps, None, "z"),
            P("z", dps),
            P(None, dps),
            P(None, dps),
        ),
        out_specs=(
            P(dps, "z", None),
            P(dps, "z", None),
            P(dps, None, "z"),
            P("z", dps),
            P(dps, None, "z"),
            P("z", dps),
            P(None, dps + ("z",)),
            P(None, dps + ("z",)),
        ),
        check_vma=False,
    )
```
